512 devices in a mesh: oi: 16 (over z), oj: 32 (over y, x, core).
Axes of the slice: x: 4, y: 4, z: 16, core: 2. Of those that a mesh axis runs over, the one named last changes fastest.
Arguments:
- amplitudes: bfloat16 [12288, 128, 128], P(('oi', 'oj')), may hold values from -6 to 6
- exchange_ints: bfloat16 [12288, 128, 128], P(('oi', 'oj')), may hold values from -6 to 6
- row_intersection: bfloat16 [12288, 128, 128], P(('oi', 'oj')), may hold values from -0.5 to 0.5
- col_intersection: bfloat16 [12288, 128, 128], P(('oi', 'oj')), may hold values from -0.5 to 0.5
- pno_energy: float32 [12288, 128], P(('oi', 'oj')), may hold values from 0.2 to 1
- row_fock: float32 [12288], P(('oi', 'oj')), may hold values from -1 to 1
- col_fock: float32 [12288], P(('oi', 'oj')), may hold values from -1 to 1
- pair_occ: int32 [12288, 2], P(('oi', 'oj')), may hold values from 0 to 19999
- fock_occ: float32 [20000], replicated, may hold values from -0.6 to -0.2
- row_peer: int32 [12288, 1], P(('oi', 'oj')), may hold values from 0 to 31; in each aligned block of 24 rows (0 to 23, 24 to 47, ...) at most 2 rows name the same one
- row_slot: int32 [12288], P(('oi', 'oj')), may hold values from 0 to 23
- col_peer: int32 [12288, 1], P(('oi', 'oj')), may hold values from 0 to 15; in each aligned block of 24 rows (0 to 23, 24 to 47, ...) at most 3 rows name the same one
- col_slot: int32 [12288], P(('oi', 'oj')), may hold values from 0 to 23
Outputs:
- new_amplitudes: bfloat16 [12288, 128, 128], P(('oi', 'oj'))
- residual: bfloat16 [12288, 128, 128], P(('oi', 'oj'))
The draws below stay inside these ranges and needn't reach their ends.
Inputs may be any that keep to these rules, and one draw needn't show every extreme that they name: `row_peer`: among the pairs of one device no index is named by more than 2 pairs, a bound that some block reaches. `col_peer`: among the pairs of one device no index is named by more than 3 pairs, a bound that some block reaches.
All inputs are finite; a program needn't handle non-finite values.
Results may differ from the reference program's by a relative error of at most 0.012.
The reference program's roundings to bfloat16 on the way count: a program that leaves them out, or rounds other values in their place, can miss the bound.
Values may be sent and summed in bfloat16 or wider, within the bound.
No kernel may reach another device: no remote copies, remote signals or barrier semaphores. Data moves between devices by JAX's collectives and lax.ppermute only.
A program may use at most 64 MiB of HBM per device.

```python
import math
import jax
import jax.numpy as jnp
import numpy as np
from jax import lax

PNO = 128
NOCC = 20000
P_DEV = 24
ITERS = 3
CAP_ROW = 2
CAP_COL = 3
PAIRS = 12288
N_OI = 16
N_OJ = 32


def plant(entries, stream_key, low, high):
    longest = entries.shape.index(max(entries.shape))
    spots = []
    for shift in (0, 1):
        where = [jax.random.randint(jax.random.fold_in(stream_key, axis), (), 0, length) for axis, length in enumerate(entries.shape)]
        where[longest] = (where[longest] + shift) % entries.shape[longest]
        spots.append(tuple(where))
    return entries.at[spots[0]].set(low).at[spots[1]].set(high)


def block_scale(own_key, shape, split, low, high):
    def one(axis_at, parts):
        heights = jax.random.uniform(jax.random.fold_in(jax.random.fold_in(own_key, 6), axis_at), (parts,), jnp.float32, low / len(split), high / len(split))
        return jnp.repeat(jnp.exp(heights), shape[axis_at] // parts).reshape((-1,) + (1,) * (len(shape) - axis_at - 1))

    gain = one(*split[0])
    for cut in split[1:]:
        gain = gain * one(*cut)
    return gain


def assign_block(own_key, own, number, rows, count, top, limit, slope):
    order = jax.random.permutation(own_key, count)
    heavy_load, usual = portions_of(count, rows * top, limit, slope, True), portions_of(count, rows * top, limit, slope, False)
    places = jnp.arange(count)

    def named(sizes, offset_by):
        used = int((sizes > 0).sum())
        fixed = max(1, used // 4)
        passed = fixed + (places - fixed + offset_by * (used - fixed)) % max(1, count - fixed)
        return jnp.zeros((count,), jnp.int32).at[order[jnp.where(places < fixed, places, passed)]].set(jnp.asarray(sizes, jnp.int32))

    sizes = jnp.where(number % 4 == 0, named(heavy_load, number // 4), named(usual, number - number // 4 - 1))
    mixed = jax.random.permutation(jax.random.fold_in(own, 3), count)
    giver, sink = mixed[0:count // 2 * 2:2], mixed[1:count // 2 * 2:2]
    room = jnp.minimum(sizes[giver] - 1, limit - sizes[sink]) // 2
    room = jnp.where((giver == order[0]) | (sink == order[0]) | (sizes[sink] == 0), 0, jnp.maximum(room, 0))
    passed = jax.random.randint(jax.random.fold_in(own, 4), (count // 2,), 0, 1 << 20) % (room + 1)
    sizes = sizes.at[giver].add(-passed).at[sink].add(passed)
    labels = jnp.searchsorted(jnp.cumsum(sizes), jnp.arange(rows * top), side="right").astype(jnp.int32)
    grid = labels.reshape(top, rows).T
    grid = grid[jax.random.permutation(jax.random.fold_in(own, 1), rows)]
    offset_by = jax.random.randint(jax.random.fold_in(own, 2), (rows, 1), 0, top)
    return jnp.take_along_axis(grid, (jnp.arange(top)[None, :] + offset_by) % top, axis=1)


def portions_of(count, total, reach, slope, full):
    portions = [(1 << 20) // math.isqrt(grade ** slope) + 1 for grade in range(1, count + 1)]
    largest = reach if full else min(reach, max(-(-total // count), total * portions[0] // sum(portions)))
    least = 1 if total - largest >= count - 1 else 0
    holding, rest = [largest] + [least] * (count - 1), total - largest - least * (count - 1)
    while rest > 0:
        free = [i for i in range(1, count) if holding[i] < largest] or [i for i in range(1, count) if holding[i] < reach]
        pool, left = sum([portions[i] for i in free]), rest
        for i in free:
            more = min(reach - holding[i], max(1, left * portions[i] // pool), rest)
            holding[i] = holding[i] + more
            rest = rest - more
    return np.array(holding)


def normal_values(own_key, dims, scale, bound, split=(), held_as=jnp.bfloat16):
    gain = block_scale(own_key, dims, split, -0.22, 0.18) if split else 1.0
    values = jax.random.normal(own_key, dims, jnp.float32) * scale * gain
    return jnp.minimum(jnp.maximum(values, -bound), bound).astype(held_as)


def setup_inputs(seed: int = 0) -> dict:
    key_of = jax.random.split(jax.random.key(seed), 14)
    amplitudes = normal_values(key_of[0], (PAIRS, PNO, PNO), 1.0, 6.0, ((0, 512),))
    exchange_ints = normal_values(key_of[1], (PAIRS, PNO, PNO), 1.0, 6.0, ((0, 512),))
    row_intersection = normal_values(key_of[2], (PAIRS, PNO, PNO), PNO ** -0.5, 0.5, ((0, 512),))
    col_intersection = normal_values(key_of[3], (PAIRS, PNO, PNO), PNO ** -0.5, 0.5, ((0, 512),))
    pno_energy = jnp.clip(jnp.exp(math.log(1.0) - 1.609438 * jax.random.uniform(key_of[4], (PAIRS, PNO), jnp.float32) ** block_scale(key_of[4], (PAIRS, PNO), ((0, 512),), -0.2, 0.2)), 0.2, 1.0)
    row_fock = jnp.clip(jax.random.uniform(key_of[5], (PAIRS,), jnp.float32, -1.0, 1.0) * block_scale(key_of[5], (PAIRS,), ((0, 512),), -0.4, 0.0), -1.0, 1.0)
    col_fock = jnp.clip(jax.random.uniform(key_of[6], (PAIRS,), jnp.float32, -1.0, 1.0) * block_scale(key_of[6], (PAIRS,), ((0, 512),), -0.4, 0.0), -1.0, 1.0)
    pair_occ = plant(jax.random.randint(key_of[7], (PAIRS, 2), 0, NOCC), jax.random.fold_in(key_of[7], 1), 0, NOCC - 1).astype(jnp.int32)
    fock_occ = jnp.clip(jax.random.uniform(key_of[8], (NOCC,), jnp.float32, -0.6, -0.2), -0.6, -0.2)
    row_peer_keys = jax.random.split(jax.random.fold_in(key_of[9], 1), PAIRS // P_DEV)
    row_peer_turns = jax.random.permutation(jax.random.fold_in(key_of[9], 3), PAIRS // P_DEV)
    row_peer = jax.vmap(lambda own, number: assign_block(jax.random.fold_in(key_of[9], 2), own, number, P_DEV, N_OJ, 1, CAP_ROW, 2))(row_peer_keys, row_peer_turns).reshape((PAIRS, 1))
    row_slot = plant(jax.random.randint(key_of[10], (PAIRS,), 0, P_DEV), jax.random.fold_in(key_of[10], 1), 0, P_DEV - 1).astype(jnp.int32)
    col_peer_keys = jax.random.split(jax.random.fold_in(key_of[11], 1), PAIRS // P_DEV)
    col_peer_turns = jax.random.permutation(jax.random.fold_in(key_of[11], 3), PAIRS // P_DEV)
    col_peer = jax.vmap(lambda own, number: assign_block(jax.random.fold_in(key_of[11], 2), own, number, P_DEV, N_OI, 1, CAP_COL, 2))(col_peer_keys, col_peer_turns).reshape((PAIRS, 1))
    col_slot = plant(jax.random.randint(key_of[12], (PAIRS,), 0, P_DEV), jax.random.fold_in(key_of[12], 1), 0, P_DEV - 1).astype(jnp.int32)
    return {"amplitudes": amplitudes, "exchange_ints": exchange_ints, "row_intersection": row_intersection, "col_intersection": col_intersection, "pno_energy": pno_energy, "row_fock": row_fock, "col_fock": col_fock, "pair_occ": pair_occ, "fock_occ": fock_occ, "row_peer": row_peer, "row_slot": row_slot, "col_peer": col_peer, "col_slot": col_slot}


def couple(blocks, intersection):
    first = jnp.einsum('pab,pbc->pac', intersection.astype(jnp.float32), blocks.astype(jnp.float32)).astype(jnp.bfloat16)
    return jnp.einsum('pac,pdc->pad', first.astype(jnp.float32), intersection.astype(jnp.float32))


def reference(amplitudes, exchange_ints, row_intersection, col_intersection, pno_energy, row_fock, col_fock, pair_occ, fock_occ, row_peer, row_slot, col_peer, col_slot):
    pair_ids = jnp.arange(PAIRS, dtype=jnp.int32)
    device = pair_ids // P_DEV
    row_source = (((device // N_OJ) * N_OJ + row_peer[:, 0]) * P_DEV + row_slot).astype(jnp.int32)
    col_source = ((col_peer[:, 0] * N_OJ + device % N_OJ) * P_DEV + col_slot).astype(jnp.int32)
    occupied = fock_occ[pair_occ[:, 0]] + fock_occ[pair_occ[:, 1]]

    def shaped(array):
        return array.reshape((N_OI * N_OJ, P_DEV) + array.shape[1:])

    stacked = tuple(shaped(array) for array in (exchange_ints, row_intersection, col_intersection, pno_energy, occupied, row_fock, col_fock, row_source, col_source))
    residual = jnp.zeros((PAIRS, PNO, PNO), jnp.bfloat16)
    for sweep in range(ITERS):
        current = amplitudes

        def one_device(item):
            ints, row_over, col_over, energy, occ_sum, row_coef, col_coef, row_from, col_from, own = item
            denominator = energy[:, :, None] + energy[:, None, :] - occ_sum[:, None, None]
            row_term = couple(current[row_from], row_over)
            col_term = couple(current[col_from], col_over)
            sweep_residual = ints.astype(jnp.float32) + denominator * own.astype(jnp.float32) - row_coef[:, None, None] * row_term - col_coef[:, None, None] * col_term
            updated = (own.astype(jnp.float32) - sweep_residual / denominator).astype(jnp.bfloat16)
            return updated, sweep_residual.astype(jnp.bfloat16)

        updated, rounded = lax.map(one_device, stacked + (shaped(amplitudes),))
        amplitudes = updated.reshape(PAIRS, PNO, PNO)
        residual = rounded.reshape(PAIRS, PNO, PNO)
    return amplitudes, residual
```

```python
import jax
import jax.numpy as jnp
from jax import lax
from jax.sharding import PartitionSpec as P

ITERS = 3
LANES = 4
STEPS = (
    ((2, 1), (2, 3)),
    ((1, 2), (3, 2)),
    ((0, 0), (2, 2)),
    ((0, 2), (2, 0)),
    ((1, 1), (3, 3)),
    ((1, 3), (3, 1)),
    ((1, 0), (3, 0)),
    ((0, 1), (0, 3)),
)


def couple(blocks, intersection):
    first = jnp.einsum(
        "pab,pbc->pac", intersection, blocks, preferred_element_type=jnp.float32
    ).astype(jnp.bfloat16)
    return jnp.einsum("pac,pdc->pad", first, intersection, preferred_element_type=jnp.float32)


def layout(peer, slot, peer_count, capacity):
    marker = (peer[:, None] == jnp.arange(peer_count, dtype=jnp.int32)[None, :]).astype(jnp.int32)
    before = jnp.sum((jnp.cumsum(marker, axis=0) - marker) * marker, axis=1)
    target = peer * capacity + before
    slot_table = jnp.zeros((peer_count * capacity,), jnp.int32).at[target].set(slot)
    return (target, slot_table.reshape(peer_count, capacity))


def ranks(peer):
    order = jnp.arange(peer.shape[0], dtype=jnp.int32)
    earlier = (peer[:, None] == peer[None, :]) & (order[None, :] < order[:, None])
    return jnp.sum(earlier.astype(jnp.int32), axis=1)


def row_requests(row_peer, row_slot, me, capacity):
    codes = lax.all_gather(row_peer * 32 + row_slot, "oj")
    mine = codes // 32 == me
    order = jnp.arange(codes.shape[1], dtype=jnp.int32)
    lower = (order[:, None] < order[None, :]).astype(jnp.float32)
    rank = jnp.dot(mine.astype(jnp.float32), lower).astype(jnp.int32)
    wants = mine[:, :, None] & (rank[:, :, None] == jnp.arange(capacity, dtype=jnp.int32))
    return jnp.sum(jnp.where(wants, (codes % 32)[:, :, None], 0), axis=1)


def core_exchange(blocks):
    return lax.ppermute(blocks, "oj", [(source, source ^ 1) for source in range(32)])


def chip_exchange(blocks, offsets):
    pairs = []
    for source in range(32):
        y, x, c = source // 8, source // 2 % 4, source % 2
        step_y, step_x = offsets[c]
        pairs.append((source, (y + step_y) % 4 * 8 + (x + step_x) % 4 * 2 + c))
    return lax.ppermute(blocks, "oj", pairs)


def row_plan(row_wanted, row_peer, rank, me):
    my_y, my_x, my_c = me // 8, me // 2 % 4, me % 2
    step_y = jnp.array([[offsets[0] for offsets in step] for step in STEPS], jnp.int32)
    step_x = jnp.array([[offsets[1] for offsets in step] for step in STEPS], jnp.int32)
    dest = (my_y + step_y) % 4 * 8 + (my_x + step_x) % 4 * 2
    core = jnp.arange(2, dtype=jnp.int32)
    dest = dest[:, :, None] + (core[None, :, None] ^ core[None, None, :])
    slots = row_wanted[dest]
    near = jnp.where(my_c == 0, slots[:, 0], slots[:, 1]).reshape(-1)
    far = jnp.where(my_c == 0, slots[:, 1], slots[:, 0]).reshape(-1)
    off = (my_y - row_peer // 8) % 4 * 4 + (my_x - row_peer // 2) % 4
    match = off[:, None, None] == (step_y * 4 + step_x)[None, :, :]
    number = jnp.arange(len(STEPS), dtype=jnp.int32)
    step = jnp.sum(jnp.where(match, number[None, :, None], 0), axis=(1, 2))
    carrier = jnp.sum(jnp.where(match, core[None, None, :], 0), axis=(1, 2))
    target = (carrier ^ my_c) * 32 + step * 4 + (carrier ^ (row_peer % 2)) * 2 + rank
    return near, far, target


def row_exchange(near, far, width):
    count = len(STEPS)
    near = near.reshape(count, 4, width, width)
    far = core_exchange(far).reshape(count, 4, width, width)
    joined = jnp.concatenate([near, far], axis=1)
    arrived = []
    for number, offsets in enumerate(STEPS):
        outgoing = joined[number]
        if number >= LANES:
            outgoing, _ = lax.optimization_barrier((outgoing, arrived[-LANES]))
        arrived.append(chip_exchange(outgoing, offsets))
    arrived = [piece.reshape(2, 2, 2, width, width) for piece in arrived]
    keep = jnp.concatenate([piece[:, 0].reshape(4, width, width) for piece in arrived], axis=0)
    swap = jnp.concatenate([piece[:, 1].reshape(4, width, width) for piece in arrived], axis=0)
    return jnp.concatenate([keep, core_exchange(swap)], axis=0)


def body(
    amplitudes,
    exchange_ints,
    row_intersection,
    col_intersection,
    pno_energy,
    row_fock,
    col_fock,
    pair_occ,
    fock_occ,
    row_peer,
    row_slot,
    col_peer,
    col_slot,
):
    width = amplitudes.shape[1]
    row_capacity, col_capacity = 2, 3
    me = lax.axis_index("oj")
    col_target, col_table = layout(col_peer[:, 0], col_slot, lax.axis_size("oi"), col_capacity)
    col_wanted = lax.all_to_all(col_table, "oi", split_axis=0, concat_axis=0, tiled=True)
    row_wanted = row_requests(row_peer[:, 0], row_slot, me, row_capacity)
    near_wanted, far_wanted, row_target = row_plan(
        row_wanted, row_peer[:, 0], ranks(row_peer[:, 0]), me
    )
    matches = (
        pair_occ.reshape(-1)[:, None] == jnp.arange(fock_occ.shape[0], dtype=jnp.int32)[None, :]
    )
    picked = jnp.sum(jnp.where(matches, fock_occ[None, :], 0.0), axis=1).reshape(-1, 2)
    occupied = picked[:, 0] + picked[:, 1]
    denominator = pno_energy[:, :, None] + pno_energy[:, None, :] - occupied[:, None, None]
    ints_wide = exchange_ints.astype(jnp.float32)
    current = amplitudes
    residual = jnp.zeros(amplitudes.shape, jnp.float32)
    for sweep in range(ITERS):
        col_fetched = lax.all_to_all(
            current[col_wanted], "oi", split_axis=0, concat_axis=0, tiled=True
        )
        row_fetched = row_exchange(current[near_wanted], current[far_wanted], width)
        row_term = couple(row_fetched[row_target], row_intersection)
        col_term = couple(col_fetched.reshape(-1, width, width)[col_target], col_intersection)
        own_wide = current.astype(jnp.float32)
        residual = (
            ints_wide
            + denominator * own_wide
            - row_fock[:, None, None] * row_term
            - col_fock[:, None, None] * col_term
        )
        current = (own_wide - residual / denominator).astype(jnp.bfloat16)
    return (current, residual.astype(jnp.bfloat16))


def solution(mesh):
    return jax.shard_map(
        body,
        mesh=mesh,
        in_specs=(
            P(("oi", "oj"), None, None),
            P(("oi", "oj"), None, None),
            P(("oi", "oj"), None, None),
            P(("oi", "oj"), None, None),
            P(("oi", "oj"), None),
            P(("oi", "oj")),
            P(("oi", "oj")),
            P(("oi", "oj"), None),
            P(),
            P(("oi", "oj"), None),
            P(("oi", "oj")),
            P(("oi", "oj"), None),
            P(("oi", "oj")),
        ),
        out_specs=(P(("oi", "oj"), None, None), P(("oi", "oj"), None, None)),
        check_vma=False,
    )
```

```python
import jax
import jax.numpy as jnp
from jax import lax
from jax.experimental import pallas as pl
from jax.experimental.pallas import tpu as pltpu
from jax.sharding import PartitionSpec as P

ITERS = 3
LANES = 4
STEPS = (
    ((2, 1), (2, 3)),
    ((1, 2), (3, 2)),
    ((0, 0), (2, 2)),
    ((0, 2), (2, 0)),
    ((1, 1), (3, 3)),
    ((1, 3), (3, 1)),
    ((1, 0), (3, 0)),
    ((0, 1), (0, 3)),
)


def couple(blocks, intersection):
    first = jnp.einsum(
        "pab,pbc->pac", intersection, blocks, preferred_element_type=jnp.float32
    ).astype(jnp.bfloat16)
    return jnp.einsum("pac,pdc->pad", first, intersection, preferred_element_type=jnp.float32)


def ranks(peer):
    order = jnp.arange(peer.shape[0], dtype=jnp.int32)
    earlier = (peer[:, None] == peer[None, :]) & (order[None, :] < order[:, None])
    return jnp.sum(earlier.astype(jnp.int32), axis=1)


def request_table(peer, slot, rank, peer_count, capacity):
    place = jnp.arange(peer_count * capacity, dtype=jnp.int32)
    hit = (peer * capacity + rank)[None, :] == place[:, None]
    return jnp.sum(jnp.where(hit, slot[None, :], 0), axis=1).reshape(peer_count, capacity)


def gather_requests(peer, slot):
    packed = jnp.pad((peer * 32 + slot)[None, :], ((0, 7), (0, 128 - peer.shape[0])), constant_values=-1)
    return lax.all_gather(packed, "oj", tiled=True)


def row_requests_kernel(codes_ref, me_ref, dest_ref, out_ref):
    codes = codes_ref[...].reshape(32, 8, 128)[:, 0, :]
    mine = (codes >> 5) == me_ref[0]
    above = lax.broadcasted_iota(jnp.int32, (128, 128), 0)
    below = lax.broadcasted_iota(jnp.int32, (128, 128), 1)
    lower = jnp.where(above < below, 1.0, 0.0).astype(jnp.bfloat16)
    marks = jnp.where(mine, 1.0, 0.0)
    rank = jnp.dot(marks.astype(jnp.bfloat16), lower, preferred_element_type=jnp.float32)
    slot = (codes & 31).astype(jnp.float32) * marks
    first = jnp.sum(jnp.where(rank < 0.5, slot, 0.0), axis=1, keepdims=True)
    second = jnp.sum(jnp.where(rank > 0.5, slot, 0.0), axis=1, keepdims=True)
    places = out_ref.shape[1]
    device = lax.broadcasted_iota(jnp.int32, (32, places), 0)
    odd = lax.broadcasted_iota(jnp.int32, (32, places), 1) & 1
    picked = jnp.where(odd == 0, first, second)
    picked = jnp.where(device == dest_ref[...], picked, 0.0)
    out_ref[...] = jnp.sum(picked, axis=0, keepdims=True).astype(jnp.int32)


def row_requests(codes, me, dest):
    return pl.pallas_call(
        row_requests_kernel,
        out_shape=jax.ShapeDtypeStruct(dest.shape, jnp.int32),
        in_specs=[
            pl.BlockSpec(memory_space=pltpu.VMEM),
            pl.BlockSpec(memory_space=pltpu.SMEM),
            pl.BlockSpec(memory_space=pltpu.VMEM),
        ],
        out_specs=pl.BlockSpec(memory_space=pltpu.VMEM),
        name="row_requests",
    )(codes, me.reshape(1), dest)


def core_exchange(blocks):
    return lax.ppermute(blocks, "oj", [(source, source ^ 1) for source in range(32)])


def chip_exchange(blocks, offsets):
    pairs = []
    for source in range(32):
        y, x, c = source // 8, source // 2 % 4, source % 2
        step_y, step_x = offsets[c]
        pairs.append((source, (y + step_y) % 4 * 8 + (x + step_x) % 4 * 2 + c))
    return lax.ppermute(blocks, "oj", pairs)


def row_plan(row_peer, rank, me, capacity):
    my_y, my_x, my_c = me // 8, me // 2 % 4, me % 2
    step_y = jnp.array([[offsets[0] for offsets in step] for step in STEPS], jnp.int32)
    step_x = jnp.array([[offsets[1] for offsets in step] for step in STEPS], jnp.int32)
    dest = (my_y + step_y) % 4 * 8 + (my_x + step_x) % 4 * 2
    core = jnp.arange(2, dtype=jnp.int32)
    dest = dest[:, :, None] + (core[None, :, None] ^ core[None, None, :])
    near = jnp.where(my_c == 0, dest[:, 0], dest[:, 1]).reshape(-1)
    far = jnp.where(my_c == 0, dest[:, 1], dest[:, 0]).reshape(-1)
    dest = jnp.repeat(jnp.concatenate([near, far]), capacity)[None, :]
    off = (my_y - row_peer // 8) % 4 * 4 + (my_x - row_peer // 2) % 4
    match = off[:, None, None] == (step_y * 4 + step_x)[None, :, :]
    number = jnp.arange(len(STEPS), dtype=jnp.int32)
    step = jnp.sum(jnp.where(match, number[None, :, None], 0), axis=(1, 2))
    carrier = jnp.sum(jnp.where(match, core[None, None, :], 0), axis=(1, 2))
    target = (carrier ^ my_c) * 32 + step * 4 + (carrier ^ (row_peer % 2)) * 2 + rank
    return dest, target


def row_exchange(near, far, width):
    count = len(STEPS)
    near = near.reshape(count, 4, width, width)
    far = core_exchange(far).reshape(count, 4, width, width)
    joined = jnp.concatenate([near, far], axis=1)
    arrived = []
    for number, offsets in enumerate(STEPS):
        outgoing = joined[number]
        if number >= LANES:
            outgoing, _ = lax.optimization_barrier((outgoing, arrived[-LANES]))
        arrived.append(chip_exchange(outgoing, offsets))
    arrived = [piece.reshape(2, 2, 2, width, width) for piece in arrived]
    keep = jnp.concatenate([piece[:, 0].reshape(4, width, width) for piece in arrived], axis=0)
    swap = jnp.concatenate([piece[:, 1].reshape(4, width, width) for piece in arrived], axis=0)
    return jnp.concatenate([keep, core_exchange(swap)], axis=0)


def body(
    amplitudes,
    exchange_ints,
    row_intersection,
    col_intersection,
    pno_energy,
    row_fock,
    col_fock,
    pair_occ,
    fock_occ,
    row_peer,
    row_slot,
    col_peer,
    col_slot,
):
    width = amplitudes.shape[1]
    row_capacity, col_capacity = 2, 3
    me = lax.axis_index("oj")
    col_rank = ranks(col_peer[:, 0])
    col_target = col_peer[:, 0] * col_capacity + col_rank
    col_table = request_table(col_peer[:, 0], col_slot, col_rank, lax.axis_size("oi"), col_capacity)
    col_wanted = lax.all_to_all(col_table, "oi", split_axis=0, concat_axis=0, tiled=True)
    codes = gather_requests(row_peer[:, 0], row_slot)
    row_dest, row_target = row_plan(row_peer[:, 0], ranks(row_peer[:, 0]), me, row_capacity)
    col_send = amplitudes[col_wanted]
    codes, col_send = lax.optimization_barrier((codes, col_send))
    wanted = row_requests(codes, me, row_dest)
    near_wanted, far_wanted = wanted[0, : wanted.shape[1] // 2], wanted[0, wanted.shape[1] // 2 :]
    matches = (
        pair_occ.reshape(-1)[:, None] == jnp.arange(fock_occ.shape[0], dtype=jnp.int32)[None, :]
    )
    picked = jnp.sum(jnp.where(matches, fock_occ[None, :], 0.0), axis=1).reshape(-1, 2)
    occupied = picked[:, 0] + picked[:, 1]
    denominator = pno_energy[:, :, None] + pno_energy[:, None, :] - occupied[:, None, None]
    ints_wide = exchange_ints.astype(jnp.float32)
    current = amplitudes
    residual = jnp.zeros(amplitudes.shape, jnp.float32)
    for sweep in range(ITERS):
        if sweep:
            col_send = current[col_wanted]
        col_fetched = lax.all_to_all(col_send, "oi", split_axis=0, concat_axis=0, tiled=True)
        row_fetched = row_exchange(current[near_wanted], current[far_wanted], width)
        row_term = couple(row_fetched[row_target], row_intersection)
        col_term = couple(col_fetched.reshape(-1, width, width)[col_target], col_intersection)
        own_wide = current.astype(jnp.float32)
        residual = (
            ints_wide
            + denominator * own_wide
            - row_fock[:, None, None] * row_term
            - col_fock[:, None, None] * col_term
        )
        current = (own_wide - residual / denominator).astype(jnp.bfloat16)
    return (current, residual.astype(jnp.bfloat16))


def solution(mesh):
    return jax.shard_map(
        body,
        mesh=mesh,
        in_specs=(
            P(("oi", "oj"), None, None),
            P(("oi", "oj"), None, None),
            P(("oi", "oj"), None, None),
            P(("oi", "oj"), None, None),
            P(("oi", "oj"), None),
            P(("oi", "oj")),
            P(("oi", "oj")),
            P(("oi", "oj"), None),
            P(),
            P(("oi", "oj"), None),
            P(("oi", "oj")),
            P(("oi", "oj"), None),
            P(("oi", "oj")),
        ),
        out_specs=(P(("oi", "oj"), None, None), P(("oi", "oj"), None, None)),
        check_vma=False,
    )
```

```python
import jax
import jax.numpy as jnp
from jax import lax
from jax.experimental import pallas as pl
from jax.experimental.pallas import tpu as pltpu
from jax.sharding import PartitionSpec as P

ITERS = 3
LANES = 4
STEPS = (
    ((2, 1), (2, 3)),
    ((1, 2), (3, 2)),
    ((0, 0), (2, 2)),
    ((0, 2), (2, 0)),
    ((1, 1), (3, 3)),
    ((1, 3), (3, 1)),
    ((1, 0), (3, 0)),
    ((0, 1), (0, 3)),
)


def couple(blocks, intersection):
    first = jnp.einsum(
        "pab,pbc->pac", intersection, blocks, preferred_element_type=jnp.float32
    ).astype(jnp.bfloat16)
    return jnp.einsum("pac,pdc->pad", first, intersection, preferred_element_type=jnp.float32)


def layout(peer, slot, peer_count, capacity):
    marker = (peer[:, None] == jnp.arange(peer_count, dtype=jnp.int32)[None, :]).astype(jnp.int32)
    before = jnp.sum((jnp.cumsum(marker, axis=0) - marker) * marker, axis=1)
    target = peer * capacity + before
    slot_table = jnp.zeros((peer_count * capacity,), jnp.int32).at[target].set(slot)
    return (target, slot_table.reshape(peer_count, capacity))


def ranks(peer):
    order = jnp.arange(peer.shape[0], dtype=jnp.int32)
    earlier = (peer[:, None] == peer[None, :]) & (order[None, :] < order[:, None])
    return jnp.sum(earlier.astype(jnp.int32), axis=1)


def row_requests(row_peer, row_slot, me, capacity):
    codes = lax.all_gather(row_peer * 32 + row_slot, "oj")
    mine = codes // 32 == me
    order = jnp.arange(codes.shape[1], dtype=jnp.int32)
    lower = (order[:, None] < order[None, :]).astype(jnp.float32)
    rank = jnp.dot(mine.astype(jnp.float32), lower).astype(jnp.int32)
    wants = mine[:, :, None] & (rank[:, :, None] == jnp.arange(capacity, dtype=jnp.int32))
    return jnp.sum(jnp.where(wants, (codes % 32)[:, :, None], 0), axis=1)


def core_exchange(blocks):
    return lax.ppermute(blocks, "oj", [(source, source ^ 1) for source in range(32)])


def chip_exchange(blocks, offsets):
    pairs = []
    for source in range(32):
        y, x, c = source // 8, source // 2 % 4, source % 2
        step_y, step_x = offsets[c]
        pairs.append((source, (y + step_y) % 4 * 8 + (x + step_x) % 4 * 2 + c))
    return lax.ppermute(blocks, "oj", pairs)


def row_plan(row_wanted, row_peer, rank, me):
    my_y, my_x, my_c = me // 8, me // 2 % 4, me % 2
    step_y = jnp.array([[offsets[0] for offsets in step] for step in STEPS], jnp.int32)
    step_x = jnp.array([[offsets[1] for offsets in step] for step in STEPS], jnp.int32)
    dest = (my_y + step_y) % 4 * 8 + (my_x + step_x) % 4 * 2
    core = jnp.arange(2, dtype=jnp.int32)
    dest = dest[:, :, None] + (core[None, :, None] ^ core[None, None, :])
    slots = row_wanted[dest]
    near = jnp.where(my_c == 0, slots[:, 0], slots[:, 1]).reshape(-1)
    far = jnp.where(my_c == 0, slots[:, 1], slots[:, 0]).reshape(-1)
    off = (my_y - row_peer // 8) % 4 * 4 + (my_x - row_peer // 2) % 4
    match = off[:, None, None] == (step_y * 4 + step_x)[None, :, :]
    number = jnp.arange(len(STEPS), dtype=jnp.int32)
    step = jnp.sum(jnp.where(match, number[None, :, None], 0), axis=(1, 2))
    carrier = jnp.sum(jnp.where(match, core[None, None, :], 0), axis=(1, 2))
    target = (carrier ^ my_c) * 32 + step * 4 + (carrier ^ (row_peer % 2)) * 2 + rank
    return near, far, target


def row_exchange(near, far, width):
    count = len(STEPS)
    near = near.reshape(count, 4, width, width)
    far = core_exchange(far).reshape(count, 4, width, width)
    joined = jnp.concatenate([near, far], axis=1)
    arrived = []
    for number, offsets in enumerate(STEPS):
        outgoing = joined[number]
        if number >= LANES:
            outgoing, _ = lax.optimization_barrier((outgoing, arrived[-LANES]))
        arrived.append(chip_exchange(outgoing, offsets))
    arrived = [piece.reshape(2, 2, 2, width, width) for piece in arrived]
    keep = jnp.concatenate([piece[:, 0].reshape(4, width, width) for piece in arrived], axis=0)
    swap = jnp.concatenate([piece[:, 1].reshape(4, width, width) for piece in arrived], axis=0)
    return jnp.concatenate([keep, core_exchange(swap)], axis=0)


def finish_kernel(
    target_ref,
    wanted_ref,
    occupied_ref,
    fock_ref,
    fetched_ref,
    inter_ref,
    base_ref,
    own_ref,
    energy_ref,
    energy_t_ref,
    new_ref,
    second_ref,
    block_ref,
    in_sem,
    out_sem,
):
    pairs = own_ref.shape[0]
    arrivals = []
    for pair in range(pairs):
        arrivals.append(
            pltpu.make_async_copy(
                fetched_ref.at[target_ref[pair]], block_ref.at[pair], in_sem.at[pair]
            )
        )
        arrivals[-1].start()
    for pair in range(pairs):
        inter = inter_ref[pair]
        arrivals[pair].wait()
        first = jnp.dot(inter, block_ref[pair], preferred_element_type=jnp.float32)
        term = lax.dot_general(
            first.astype(jnp.bfloat16),
            inter,
            (((1,), (1,)), ((), ())),
            preferred_element_type=jnp.float32,
        )
        denominator = (
            energy_t_ref[:, pair : pair + 1] + energy_ref[pair : pair + 1, :] - occupied_ref[pair]
        )
        residual = base_ref[pair] - fock_ref[pair] * term
        new = own_ref[pair].astype(jnp.float32) - residual / denominator
        new_ref[pair] = new.astype(jnp.bfloat16)
        if out_sem is None:
            second_ref[pair] = residual.astype(jnp.bfloat16)
    if out_sem is not None:
        sends = []
        for place in range(second_ref.shape[0]):
            sends.append(
                pltpu.make_async_copy(
                    new_ref.at[wanted_ref[place]], second_ref.at[place], out_sem.at[place]
                )
            )
            sends[-1].start()
        for send in sends:
            send.wait()


def last_kernel(*refs):
    finish_kernel(*refs, None)


def finish(target, wanted, occupied, fock, fetched, inter, base, own, energy, last):
    pairs = own.shape[0]
    smem, vmem = pl.BlockSpec(memory_space=pltpu.SMEM), pl.BlockSpec(memory_space=pltpu.VMEM)
    hbm = pl.BlockSpec(memory_space=pltpu.HBM)
    scratch = [pltpu.VMEM(own.shape, jnp.bfloat16), pltpu.SemaphoreType.DMA((pairs,))]
    if not last:
        scratch.append(pltpu.SemaphoreType.DMA((fetched.shape[0],)))
    if last:
        second_shape = jax.ShapeDtypeStruct(own.shape, jnp.bfloat16)
    else:
        second_shape = pltpu.HBM(fetched.shape, jnp.bfloat16)
    return pl.pallas_call(
        last_kernel if last else finish_kernel,
        out_shape=(
            jax.ShapeDtypeStruct(own.shape, jnp.bfloat16),
            second_shape,
        ),
        in_specs=[smem] * 4 + [hbm] + [vmem] * 5,
        out_specs=(vmem, vmem if last else hbm),
        scratch_shapes=scratch,
        compiler_params=pltpu.CompilerParams(vmem_limit_bytes=24 * 2**20),
        name="finish_last" if last else "finish",
    )(target, wanted, occupied, fock, fetched, inter, base, own, energy, energy.T)


def body(
    amplitudes,
    exchange_ints,
    row_intersection,
    col_intersection,
    pno_energy,
    row_fock,
    col_fock,
    pair_occ,
    fock_occ,
    row_peer,
    row_slot,
    col_peer,
    col_slot,
):
    width = amplitudes.shape[1]
    row_capacity, col_capacity = 2, 3
    me = lax.axis_index("oj")
    col_target, col_table = layout(col_peer[:, 0], col_slot, lax.axis_size("oi"), col_capacity)
    col_wanted = lax.all_to_all(col_table, "oi", split_axis=0, concat_axis=0, tiled=True)
    row_wanted = row_requests(row_peer[:, 0], row_slot, me, row_capacity)
    near_wanted, far_wanted, row_target = row_plan(
        row_wanted, row_peer[:, 0], ranks(row_peer[:, 0]), me
    )
    matches = (
        pair_occ.reshape(-1)[:, None] == jnp.arange(fock_occ.shape[0], dtype=jnp.int32)[None, :]
    )
    picked = jnp.sum(jnp.where(matches, fock_occ[None, :], 0.0), axis=1).reshape(-1, 2)
    occupied = picked[:, 0] + picked[:, 1]
    denominator = pno_energy[:, :, None] + pno_energy[:, None, :] - occupied[:, None, None]
    ints_wide = exchange_ints.astype(jnp.float32)
    current = amplitudes
    col_send = current[col_wanted.reshape(-1)]
    for sweep in range(ITERS):
        col_fetched = lax.all_to_all(col_send, "oi", split_axis=0, concat_axis=0, tiled=True)
        row_fetched = row_exchange(current[near_wanted], current[far_wanted], width)
        row_term = couple(row_fetched[row_target], row_intersection)
        base = (
            ints_wide
            + denominator * current.astype(jnp.float32)
            - row_fock[:, None, None] * row_term
        )
        current, col_send = finish(
            col_target,
            col_wanted.reshape(-1),
            occupied,
            col_fock,
            col_fetched.reshape(-1, width, width),
            col_intersection,
            base,
            current,
            pno_energy,
            sweep == ITERS - 1,
        )
    return (current, col_send)


def solution(mesh):
    return jax.shard_map(
        body,
        mesh=mesh,
        in_specs=(
            P(("oi", "oj"), None, None),
            P(("oi", "oj"), None, None),
            P(("oi", "oj"), None, None),
            P(("oi", "oj"), None, None),
            P(("oi", "oj"), None),
            P(("oi", "oj")),
            P(("oi", "oj")),
            P(("oi", "oj"), None),
            P(),
            P(("oi", "oj"), None),
            P(("oi", "oj")),
            P(("oi", "oj"), None),
            P(("oi", "oj")),
        ),
        out_specs=(P(("oi", "oj"), None, None), P(("oi", "oj"), None, None)),
        check_vma=False,
    )
```

```python
import jax
import jax.numpy as jnp
from jax import lax
from jax.experimental import pallas as pl
from jax.experimental.pallas import tpu as pltpu
from jax.sharding import PartitionSpec as P

ITERS = 3
GROUP = 8
LANES = 4
STEPS = (
    ((2, 1), (2, 3)),
    ((1, 2), (3, 2)),
    ((0, 0), (2, 2)),
    ((0, 2), (2, 0)),
    ((1, 1), (3, 3)),
    ((1, 3), (3, 1)),
    ((1, 0), (3, 0)),
    ((0, 1), (0, 3)),
)


def couple(blocks, intersection):
    first = jnp.einsum(
        "pab,pbc->pac", intersection, blocks, preferred_element_type=jnp.float32
    ).astype(jnp.bfloat16)
    return jnp.einsum("pac,pdc->pad", first, intersection, preferred_element_type=jnp.float32)


def ranks(peer):
    order = jnp.arange(peer.shape[0], dtype=jnp.int32)
    earlier = (peer[:, None] == peer[None, :]) & (order[None, :] < order[:, None])
    return jnp.sum(earlier.astype(jnp.int32), axis=1)


def request_table(peer, slot, rank, peer_count, capacity):
    place = jnp.arange(peer_count * capacity, dtype=jnp.int32)
    hit = (peer * capacity + rank)[None, :] == place[:, None]
    return jnp.sum(jnp.where(hit, slot[None, :], 0), axis=1).reshape(peer_count, capacity)


def row_requests(row_peer, row_slot, me, capacity):
    codes = lax.all_gather(row_peer * 32 + row_slot, "oj")
    mine = codes // 32 == me
    order = jnp.arange(codes.shape[1], dtype=jnp.int32)
    lower = (order[:, None] < order[None, :]).astype(jnp.float32)
    rank = jnp.dot(mine.astype(jnp.float32), lower).astype(jnp.int32)
    wants = mine[:, :, None] & (rank[:, :, None] == jnp.arange(capacity, dtype=jnp.int32))
    return jnp.sum(jnp.where(wants, (codes % 32)[:, :, None], 0), axis=1)


def core_exchange(blocks):
    return lax.ppermute(blocks, "oj", [(source, source ^ 1) for source in range(32)])


def chip_exchange(blocks, offsets):
    pairs = []
    for source in range(32):
        y, x, c = source // 8, source // 2 % 4, source % 2
        step_y, step_x = offsets[c]
        pairs.append((source, (y + step_y) % 4 * 8 + (x + step_x) % 4 * 2 + c))
    return lax.ppermute(blocks, "oj", pairs)


def row_plan(row_wanted, row_peer, rank, me):
    my_y, my_x, my_c = me // 8, me // 2 % 4, me % 2
    step_y = jnp.array([[offsets[0] for offsets in step] for step in STEPS], jnp.int32)
    step_x = jnp.array([[offsets[1] for offsets in step] for step in STEPS], jnp.int32)
    dest = (my_y + step_y) % 4 * 8 + (my_x + step_x) % 4 * 2
    core = jnp.arange(2, dtype=jnp.int32)
    dest = dest[:, :, None] + (core[None, :, None] ^ core[None, None, :])
    slots = row_wanted[dest]
    near = jnp.where(my_c == 0, slots[:, 0], slots[:, 1]).reshape(-1)
    far = jnp.where(my_c == 0, slots[:, 1], slots[:, 0]).reshape(-1)
    off = (my_y - row_peer // 8) % 4 * 4 + (my_x - row_peer // 2) % 4
    match = off[:, None, None] == (step_y * 4 + step_x)[None, :, :]
    number = jnp.arange(len(STEPS), dtype=jnp.int32)
    step = jnp.sum(jnp.where(match, number[None, :, None], 0), axis=(1, 2))
    carrier = jnp.sum(jnp.where(match, core[None, None, :], 0), axis=(1, 2))
    target = (carrier ^ my_c) * 32 + step * 4 + (carrier ^ (row_peer % 2)) * 2 + rank
    return near, far, target


def row_exchange(near, far, width):
    count = len(STEPS)
    near = near.reshape(count, 4, width, width)
    far = core_exchange(far).reshape(count, 4, width, width)
    joined = jnp.concatenate([near, far], axis=1)
    arrived = []
    for number, offsets in enumerate(STEPS):
        outgoing = joined[number]
        if number >= LANES:
            outgoing, _ = lax.optimization_barrier((outgoing, arrived[-LANES]))
        arrived.append(chip_exchange(outgoing, offsets))
    arrived = [piece.reshape(2, 2, 2, width, width) for piece in arrived]
    keep = jnp.concatenate([piece[:, 0].reshape(4, width, width) for piece in arrived], axis=0)
    swap = jnp.concatenate([piece[:, 1].reshape(4, width, width) for piece in arrived], axis=0)
    return jnp.concatenate([keep, core_exchange(swap)], axis=0)


def finish_kernel(
    target_ref,
    wanted_ref,
    occupied_ref,
    fock_ref,
    energy_ref,
    energy_t_ref,
    fetched_ref,
    inter_ref,
    base_ref,
    own_ref,
    new_ref,
    second_ref,
    block_scr,
    inter_scr,
    base_scr,
    own_scr,
    new_scr,
    second_scr,
    in_sem,
    group_sem,
    out_sem,
    send_sem,
):
    pairs = own_scr.shape[0]
    last = send_sem is None
    groups = [(start, min(GROUP, pairs - start)) for start in range(0, pairs, GROUP)]
    waits = []
    for number, (start, size) in enumerate(groups):
        copies = [
            pltpu.make_async_copy(
                source.at[pl.ds(start, size)],
                buffer.at[pl.ds(start, size)],
                group_sem.at[kind, number],
            )
            for kind, (source, buffer) in enumerate(
                ((inter_ref, inter_scr), (own_ref, own_scr), (base_ref, base_scr))
            )
        ]
        for pair in range(start, start + size):
            copies.append(
                pltpu.make_async_copy(
                    fetched_ref.at[target_ref[pair]], block_scr.at[pair], in_sem.at[pair]
                )
            )
        for copy in copies:
            copy.start()
        waits.append(copies)
    leaving = []
    for number, (start, size) in enumerate(groups):
        for copy in waits[number]:
            copy.wait()
        group = range(start, start + size)
        firsts = [
            jnp.dot(inter_scr[pair], block_scr[pair], preferred_element_type=jnp.float32).astype(
                jnp.bfloat16
            )
            for pair in group
        ]
        terms = [
            lax.dot_general(
                first,
                inter_scr[pair],
                (((1,), (1,)), ((), ())),
                preferred_element_type=jnp.float32,
            )
            for pair, first in zip(group, firsts)
        ]
        for pair, term in zip(group, terms):
            denominator = (
                energy_t_ref[:, pair : pair + 1]
                + energy_ref[pair : pair + 1, :]
                - occupied_ref[pair]
            )
            residual = base_scr[pair] - fock_ref[pair] * term
            new = own_scr[pair].astype(jnp.float32) - residual / denominator
            new_scr[pair] = new.astype(jnp.bfloat16)
            if last:
                second_scr[pair] = residual.astype(jnp.bfloat16)
        results = [(new_scr, new_ref)] + ([(second_scr, second_ref)] if last else [])
        for kind, (buffer, out) in enumerate(results):
            leaving.append(
                pltpu.make_async_copy(
                    buffer.at[pl.ds(start, size)],
                    out.at[pl.ds(start, size)],
                    out_sem.at[kind, number],
                )
            )
            leaving[-1].start()
    if not last:
        for place in range(second_ref.shape[0]):
            leaving.append(
                pltpu.make_async_copy(
                    new_scr.at[wanted_ref[place]], second_ref.at[place], send_sem.at[place]
                )
            )
            leaving[-1].start()
    for copy in leaving:
        copy.wait()


def middle_kernel(*refs):
    finish_kernel(*refs[:17], None, *refs[17:])


def last_kernel(*refs):
    finish_kernel(*refs, None)


def finish(target, wanted, occupied, fock, fetched, inter, base, own, energy, last):
    pairs = own.shape[0]
    count = -(-pairs // GROUP)
    smem, vmem = pl.BlockSpec(memory_space=pltpu.SMEM), pl.BlockSpec(memory_space=pltpu.VMEM)
    hbm = pl.BlockSpec(memory_space=pltpu.HBM)
    narrow = pltpu.VMEM(own.shape, jnp.bfloat16)
    scratch = [narrow, narrow, pltpu.VMEM(own.shape, jnp.float32), narrow, narrow]
    if last:
        scratch.append(narrow)
    scratch += [
        pltpu.SemaphoreType.DMA((pairs,)),
        pltpu.SemaphoreType.DMA((3, count)),
        pltpu.SemaphoreType.DMA((2, count)),
    ]
    if not last:
        scratch.append(pltpu.SemaphoreType.DMA((fetched.shape[0],)))
    return pl.pallas_call(
        last_kernel if last else middle_kernel,
        out_shape=(
            pltpu.HBM(own.shape, jnp.bfloat16),
            pltpu.HBM(own.shape if last else fetched.shape, jnp.bfloat16),
        ),
        in_specs=[smem] * 4 + [vmem] * 2 + [hbm] * 4,
        out_specs=(hbm, hbm),
        scratch_shapes=scratch,
        name="finish_last" if last else "finish",
    )(target, wanted, occupied, fock, energy, energy.T, fetched, inter, base, own)


def body(
    amplitudes,
    exchange_ints,
    row_intersection,
    col_intersection,
    pno_energy,
    row_fock,
    col_fock,
    pair_occ,
    fock_occ,
    row_peer,
    row_slot,
    col_peer,
    col_slot,
):
    width = amplitudes.shape[1]
    row_capacity, col_capacity = 2, 3
    me = lax.axis_index("oj")
    col_rank = ranks(col_peer[:, 0])
    col_target = col_peer[:, 0] * col_capacity + col_rank
    col_table = request_table(col_peer[:, 0], col_slot, col_rank, lax.axis_size("oi"), col_capacity)
    col_wanted = lax.all_to_all(col_table, "oi", split_axis=0, concat_axis=0, tiled=True)
    row_wanted = row_requests(row_peer[:, 0], row_slot, me, row_capacity)
    near_wanted, far_wanted, row_target = row_plan(
        row_wanted, row_peer[:, 0], ranks(row_peer[:, 0]), me
    )
    matches = (
        pair_occ.reshape(-1)[:, None] == jnp.arange(fock_occ.shape[0], dtype=jnp.int32)[None, :]
    )
    picked = jnp.sum(jnp.where(matches, fock_occ[None, :], 0.0), axis=1).reshape(-1, 2)
    occupied = picked[:, 0] + picked[:, 1]
    denominator = pno_energy[:, :, None] + pno_energy[:, None, :] - occupied[:, None, None]
    ints_wide = exchange_ints.astype(jnp.float32)
    current = amplitudes
    col_send = current[col_wanted.reshape(-1)]
    for sweep in range(ITERS):
        col_fetched = lax.all_to_all(col_send, "oi", split_axis=0, concat_axis=0, tiled=True)
        row_fetched = row_exchange(current[near_wanted], current[far_wanted], width)
        row_term = couple(row_fetched[row_target], row_intersection)
        base = (
            ints_wide
            + denominator * current.astype(jnp.float32)
            - row_fock[:, None, None] * row_term
        )
        current, col_send = finish(
            col_target,
            col_wanted.reshape(-1),
            occupied,
            col_fock,
            col_fetched.reshape(-1, width, width),
            col_intersection,
            base,
            current,
            pno_energy,
            sweep == ITERS - 1,
        )
    return (current, col_send)


def solution(mesh):
    return jax.shard_map(
        body,
        mesh=mesh,
        in_specs=(
            P(("oi", "oj"), None, None),
            P(("oi", "oj"), None, None),
            P(("oi", "oj"), None, None),
            P(("oi", "oj"), None, None),
            P(("oi", "oj"), None),
            P(("oi", "oj")),
            P(("oi", "oj")),
            P(("oi", "oj"), None),
            P(),
            P(("oi", "oj"), None),
            P(("oi", "oj")),
            P(("oi", "oj"), None),
            P(("oi", "oj")),
        ),
        out_specs=(P(("oi", "oj"), None, None), P(("oi", "oj"), None, None)),
        check_vma=False,
    )
```

```python
import functools

import jax
import jax.numpy as jnp
from jax import lax
from jax.experimental import pallas as pl
from jax.experimental.pallas import tpu as pltpu
from jax.sharding import PartitionSpec as P

ITERS = 3
GROUP = 8
LANES = 4
STEPS = (
    ((2, 1), (2, 3)),
    ((1, 2), (3, 2)),
    ((0, 0), (2, 2)),
    ((0, 2), (2, 0)),
    ((1, 1), (3, 3)),
    ((1, 3), (3, 1)),
    ((1, 0), (3, 0)),
    ((0, 1), (0, 3)),
)


def couple(blocks, intersection):
    first = jnp.einsum(
        "pab,pbc->pac", intersection, blocks, preferred_element_type=jnp.float32
    ).astype(jnp.bfloat16)
    return jnp.einsum("pac,pdc->pad", first, intersection, preferred_element_type=jnp.float32)


def ranks(peer):
    order = jnp.arange(peer.shape[0], dtype=jnp.int32)
    earlier = (peer[:, None] == peer[None, :]) & (order[None, :] < order[:, None])
    return jnp.sum(earlier.astype(jnp.int32), axis=1)


def request_table(peer, slot, rank, peer_count, capacity):
    place = jnp.arange(peer_count * capacity, dtype=jnp.int32)
    hit = (peer * capacity + rank)[None, :] == place[:, None]
    return jnp.sum(jnp.where(hit, slot[None, :], 0), axis=1).reshape(peer_count, capacity)


def row_requests(row_peer, row_slot, me, capacity):
    codes = lax.all_gather(row_peer * 32 + row_slot, "oj")
    mine = codes // 32 == me
    order = jnp.arange(codes.shape[1], dtype=jnp.int32)
    lower = (order[:, None] < order[None, :]).astype(jnp.float32)
    rank = jnp.dot(mine.astype(jnp.float32), lower).astype(jnp.int32)
    wants = mine[:, :, None] & (rank[:, :, None] == jnp.arange(capacity, dtype=jnp.int32))
    return jnp.sum(jnp.where(wants, (codes % 32)[:, :, None], 0), axis=1)


def core_exchange(blocks):
    return lax.ppermute(blocks, "oj", [(source, source ^ 1) for source in range(32)])


def chip_exchange(blocks, offsets):
    pairs = []
    for source in range(32):
        y, x, c = source // 8, source // 2 % 4, source % 2
        step_y, step_x = offsets[c]
        pairs.append((source, (y + step_y) % 4 * 8 + (x + step_x) % 4 * 2 + c))
    return lax.ppermute(blocks, "oj", pairs)


def row_plan(row_wanted, row_peer, rank, me):
    my_y, my_x, my_c = me // 8, me // 2 % 4, me % 2
    step_y = jnp.array([[offsets[0] for offsets in step] for step in STEPS], jnp.int32)
    step_x = jnp.array([[offsets[1] for offsets in step] for step in STEPS], jnp.int32)
    dest = (my_y + step_y) % 4 * 8 + (my_x + step_x) % 4 * 2
    core = jnp.arange(2, dtype=jnp.int32)
    dest = dest[:, :, None] + (core[None, :, None] ^ core[None, None, :])
    slots = row_wanted[dest]
    near = jnp.where(my_c == 0, slots[:, 0], slots[:, 1]).reshape(-1)
    far = jnp.where(my_c == 0, slots[:, 1], slots[:, 0]).reshape(-1)
    off = (my_y - row_peer // 8) % 4 * 4 + (my_x - row_peer // 2) % 4
    match = off[:, None, None] == (step_y * 4 + step_x)[None, :, :]
    number = jnp.arange(len(STEPS), dtype=jnp.int32)
    step = jnp.sum(jnp.where(match, number[None, :, None], 0), axis=(1, 2))
    carrier = jnp.sum(jnp.where(match, core[None, None, :], 0), axis=(1, 2))
    target = (carrier ^ my_c) * 32 + step * 4 + (carrier ^ (row_peer % 2)) * 2 + rank
    return near, far, target


def row_exchange(near, far, width):
    count = len(STEPS)
    near = near.reshape(count, 4, width, width)
    far = core_exchange(far).reshape(count, 4, width, width)
    joined = jnp.concatenate([near, far], axis=1)
    arrived = []
    for number, offsets in enumerate(STEPS):
        outgoing = joined[number]
        if number >= LANES:
            outgoing, _ = lax.optimization_barrier((outgoing, arrived[-LANES]))
        arrived.append(chip_exchange(outgoing, offsets))
    swapped = core_exchange(collect(arrived, 1, None))
    return collect(arrived, 0, swapped)


def collect_kernel(*refs, part, whole):
    *pieces, out_ref, sems = refs
    copies = []
    places = [(source, first, 2) for source in pieces[: len(STEPS)] for first in (2 * part, 2 * part + 4)]
    if whole:
        places.append((pieces[-1], 0, whole))
    at = 0
    for number, (source, first, size) in enumerate(places):
        copies.append(
            pltpu.make_async_copy(
                source.at[pl.ds(first, size)], out_ref.at[pl.ds(at, size)], sems.at[number]
            )
        )
        copies[-1].start()
        at += size
    for copy in copies:
        copy.wait()


def collect(pieces, part, extra):
    whole = 0 if extra is None else extra.shape[0]
    operands = list(pieces) + ([] if extra is None else [extra])
    count = 4 * len(pieces) + whole
    hbm = pl.BlockSpec(memory_space=pltpu.HBM)
    return pl.pallas_call(
        functools.partial(collect_kernel, part=part, whole=whole),
        out_shape=pltpu.HBM((count,) + pieces[0].shape[1:], pieces[0].dtype),
        in_specs=[hbm] * len(operands),
        out_specs=hbm,
        scratch_shapes=[pltpu.SemaphoreType.DMA((2 * len(pieces) + 1,))],
        name="collect_kept" if whole else "collect_swapped",
    )(*operands)


def finish_kernel(
    target_ref,
    wanted_ref,
    occupied_ref,
    fock_ref,
    energy_ref,
    energy_t_ref,
    fetched_ref,
    inter_ref,
    base_ref,
    own_ref,
    new_ref,
    second_ref,
    block_scr,
    inter_scr,
    base_scr,
    own_scr,
    new_scr,
    second_scr,
    in_sem,
    group_sem,
    out_sem,
    send_sem,
):
    pairs = own_scr.shape[0]
    last = send_sem is None
    groups = [(start, min(GROUP, pairs - start)) for start in range(0, pairs, GROUP)]
    waits = []
    for number, (start, size) in enumerate(groups):
        copies = [
            pltpu.make_async_copy(
                source.at[pl.ds(start, size)],
                buffer.at[pl.ds(start, size)],
                group_sem.at[kind, number],
            )
            for kind, (source, buffer) in enumerate(
                ((inter_ref, inter_scr), (own_ref, own_scr), (base_ref, base_scr))
            )
        ]
        for pair in range(start, start + size):
            copies.append(
                pltpu.make_async_copy(
                    fetched_ref.at[target_ref[pair]], block_scr.at[pair], in_sem.at[pair]
                )
            )
        for copy in copies:
            copy.start()
        waits.append(copies)
    leaving = []
    for number, (start, size) in enumerate(groups):
        for copy in waits[number]:
            copy.wait()
        group = range(start, start + size)
        firsts = [
            jnp.dot(inter_scr[pair], block_scr[pair], preferred_element_type=jnp.float32).astype(
                jnp.bfloat16
            )
            for pair in group
        ]
        terms = [
            lax.dot_general(
                first,
                inter_scr[pair],
                (((1,), (1,)), ((), ())),
                preferred_element_type=jnp.float32,
            )
            for pair, first in zip(group, firsts)
        ]
        for pair, term in zip(group, terms):
            denominator = (
                energy_t_ref[:, pair : pair + 1]
                + energy_ref[pair : pair + 1, :]
                - occupied_ref[pair]
            )
            residual = base_scr[pair] - fock_ref[pair] * term
            new = own_scr[pair].astype(jnp.float32) - residual / denominator
            new_scr[pair] = new.astype(jnp.bfloat16)
            if last:
                second_scr[pair] = residual.astype(jnp.bfloat16)
        results = [(new_scr, new_ref)] + ([(second_scr, second_ref)] if last else [])
        for kind, (buffer, out) in enumerate(results):
            leaving.append(
                pltpu.make_async_copy(
                    buffer.at[pl.ds(start, size)],
                    out.at[pl.ds(start, size)],
                    out_sem.at[kind, number],
                )
            )
            leaving[-1].start()
    if not last:
        for place in range(second_ref.shape[0]):
            leaving.append(
                pltpu.make_async_copy(
                    new_scr.at[wanted_ref[place]], second_ref.at[place], send_sem.at[place]
                )
            )
            leaving[-1].start()
    for copy in leaving:
        copy.wait()


def middle_kernel(*refs):
    finish_kernel(*refs[:17], None, *refs[17:])


def last_kernel(*refs):
    finish_kernel(*refs, None)


def finish(target, wanted, occupied, fock, fetched, inter, base, own, energy, last):
    pairs = own.shape[0]
    count = -(-pairs // GROUP)
    smem, vmem = pl.BlockSpec(memory_space=pltpu.SMEM), pl.BlockSpec(memory_space=pltpu.VMEM)
    hbm = pl.BlockSpec(memory_space=pltpu.HBM)
    narrow = pltpu.VMEM(own.shape, jnp.bfloat16)
    scratch = [narrow, narrow, pltpu.VMEM(own.shape, jnp.float32), narrow, narrow]
    if last:
        scratch.append(narrow)
    scratch += [
        pltpu.SemaphoreType.DMA((pairs,)),
        pltpu.SemaphoreType.DMA((3, count)),
        pltpu.SemaphoreType.DMA((2, count)),
    ]
    if not last:
        scratch.append(pltpu.SemaphoreType.DMA((fetched.shape[0],)))
    return pl.pallas_call(
        last_kernel if last else middle_kernel,
        out_shape=(
            pltpu.HBM(own.shape, jnp.bfloat16),
            pltpu.HBM(own.shape if last else fetched.shape, jnp.bfloat16),
        ),
        in_specs=[smem] * 4 + [vmem] * 2 + [hbm] * 4,
        out_specs=(hbm, hbm),
        scratch_shapes=scratch,
        name="finish_last" if last else "finish",
    )(target, wanted, occupied, fock, energy, energy.T, fetched, inter, base, own)


def body(
    amplitudes,
    exchange_ints,
    row_intersection,
    col_intersection,
    pno_energy,
    row_fock,
    col_fock,
    pair_occ,
    fock_occ,
    row_peer,
    row_slot,
    col_peer,
    col_slot,
):
    width = amplitudes.shape[1]
    row_capacity, col_capacity = 2, 3
    me = lax.axis_index("oj")
    col_rank = ranks(col_peer[:, 0])
    col_target = col_peer[:, 0] * col_capacity + col_rank
    col_table = request_table(col_peer[:, 0], col_slot, col_rank, lax.axis_size("oi"), col_capacity)
    col_wanted = lax.all_to_all(col_table, "oi", split_axis=0, concat_axis=0, tiled=True)
    row_wanted = row_requests(row_peer[:, 0], row_slot, me, row_capacity)
    near_wanted, far_wanted, row_target = row_plan(
        row_wanted, row_peer[:, 0], ranks(row_peer[:, 0]), me
    )
    matches = (
        pair_occ.reshape(-1)[:, None] == jnp.arange(fock_occ.shape[0], dtype=jnp.int32)[None, :]
    )
    picked = jnp.sum(jnp.where(matches, fock_occ[None, :], 0.0), axis=1).reshape(-1, 2)
    occupied = picked[:, 0] + picked[:, 1]
    denominator = pno_energy[:, :, None] + pno_energy[:, None, :] - occupied[:, None, None]
    ints_wide = exchange_ints.astype(jnp.float32)
    current = amplitudes
    col_send = current[col_wanted.reshape(-1)]
    for sweep in range(ITERS):
        col_fetched = lax.all_to_all(col_send, "oi", split_axis=0, concat_axis=0, tiled=True)
        row_fetched = row_exchange(current[near_wanted], current[far_wanted], width)
        row_term = couple(row_fetched[row_target], row_intersection)
        base = (
            ints_wide
            + denominator * current.astype(jnp.float32)
            - row_fock[:, None, None] * row_term
        )
        current, col_send = finish(
            col_target,
            col_wanted.reshape(-1),
            occupied,
            col_fock,
            col_fetched.reshape(-1, width, width),
            col_intersection,
            base,
            current,
            pno_energy,
            sweep == ITERS - 1,
        )
    return (current, col_send)


def solution(mesh):
    return jax.shard_map(
        body,
        mesh=mesh,
        in_specs=(
            P(("oi", "oj"), None, None),
            P(("oi", "oj"), None, None),
            P(("oi", "oj"), None, None),
            P(("oi", "oj"), None, None),
            P(("oi", "oj"), None),
            P(("oi", "oj")),
            P(("oi", "oj")),
            P(("oi", "oj"), None),
            P(),
            P(("oi", "oj"), None),
            P(("oi", "oj")),
            P(("oi", "oj"), None),
            P(("oi", "oj")),
        ),
        out_specs=(P(("oi", "oj"), None, None), P(("oi", "oj"), None, None)),
        check_vma=False,
    )
```

```python
import functools

import jax
import jax.numpy as jnp
from jax import lax
from jax.experimental import pallas as pl
from jax.experimental.pallas import tpu as pltpu
from jax.sharding import PartitionSpec as P

ITERS = 3
GROUP = 8
LANES = 4
STEPS = (
    ((2, 1), (2, 3)),
    ((1, 2), (3, 2)),
    ((0, 0), (2, 2)),
    ((0, 2), (2, 0)),
    ((1, 1), (3, 3)),
    ((1, 3), (3, 1)),
    ((1, 0), (3, 0)),
    ((0, 1), (0, 3)),
)


def couple(blocks, intersection):
    first = jnp.einsum(
        "pab,pbc->pac", intersection, blocks, preferred_element_type=jnp.float32
    ).astype(jnp.bfloat16)
    return jnp.einsum("pac,pdc->pad", first, intersection, preferred_element_type=jnp.float32)


def ranks(peer):
    order = jnp.arange(peer.shape[0], dtype=jnp.int32)
    earlier = (peer[:, None] == peer[None, :]) & (order[None, :] < order[:, None])
    return jnp.sum(earlier.astype(jnp.int32), axis=1)


def request_table(peer, slot, rank, peer_count, capacity):
    place = jnp.arange(peer_count * capacity, dtype=jnp.int32)
    hit = (peer * capacity + rank)[None, :] == place[:, None]
    return jnp.sum(jnp.where(hit, slot[None, :], 0), axis=1).reshape(peer_count, capacity)


def row_requests(row_peer, row_slot, me, capacity):
    codes = lax.all_gather(row_peer * 32 + row_slot, "oj")
    mine = codes // 32 == me
    order = jnp.arange(codes.shape[1], dtype=jnp.int32)
    lower = (order[:, None] < order[None, :]).astype(jnp.float32)
    rank = jnp.dot(mine.astype(jnp.float32), lower).astype(jnp.int32)
    wants = mine[:, :, None] & (rank[:, :, None] == jnp.arange(capacity, dtype=jnp.int32))
    return jnp.sum(jnp.where(wants, (codes % 32)[:, :, None], 0), axis=1)


def core_exchange(blocks):
    return lax.ppermute(blocks, "oj", [(source, source ^ 1) for source in range(32)])


def chip_exchange(blocks, offsets):
    pairs = []
    for source in range(32):
        y, x, c = source // 8, source // 2 % 4, source % 2
        step_y, step_x = offsets[c]
        pairs.append((source, (y + step_y) % 4 * 8 + (x + step_x) % 4 * 2 + c))
    return lax.ppermute(blocks, "oj", pairs)


def row_plan(row_wanted, row_peer, rank, me):
    my_y, my_x, my_c = me // 8, me // 2 % 4, me % 2
    step_y = jnp.array([[offsets[0] for offsets in step] for step in STEPS], jnp.int32)
    step_x = jnp.array([[offsets[1] for offsets in step] for step in STEPS], jnp.int32)
    dest = (my_y + step_y) % 4 * 8 + (my_x + step_x) % 4 * 2
    core = jnp.arange(2, dtype=jnp.int32)
    dest = dest[:, :, None] + (core[None, :, None] ^ core[None, None, :])
    slots = row_wanted[dest]
    near = jnp.where(my_c == 0, slots[:, 0], slots[:, 1]).reshape(-1)
    far = jnp.where(my_c == 0, slots[:, 1], slots[:, 0]).reshape(-1)
    off = (my_y - row_peer // 8) % 4 * 4 + (my_x - row_peer // 2) % 4
    match = off[:, None, None] == (step_y * 4 + step_x)[None, :, :]
    number = jnp.arange(len(STEPS), dtype=jnp.int32)
    step = jnp.sum(jnp.where(match, number[None, :, None], 0), axis=(1, 2))
    carrier = jnp.sum(jnp.where(match, core[None, None, :], 0), axis=(1, 2))
    target = (carrier ^ my_c) * 32 + step * 4 + (carrier ^ (row_peer % 2)) * 2 + rank
    return near, far, target


def row_exchange(near, far, width):
    count = len(STEPS)
    near = near.reshape(count, 4, width, width)
    far = core_exchange(far).reshape(count, 4, width, width)
    joined = jnp.concatenate([near, far], axis=1)
    arrived = []
    for number, offsets in enumerate(STEPS):
        outgoing = joined[number]
        if number >= LANES:
            outgoing, _ = lax.optimization_barrier((outgoing, arrived[-LANES]))
        arrived.append(chip_exchange(outgoing, offsets))
    swapped = core_exchange(collect(arrived, 1, None))
    return collect(arrived, 0, swapped)


def collect_kernel(*refs, part, whole):
    *pieces, out_ref, buffer, sems = refs
    copies = []
    places = [(source, first, 2) for source in pieces[: len(STEPS)] for first in (2 * part, 2 * part + 4)]
    if whole:
        places.append((pieces[-1], 0, whole))
    at = 0
    for number, (source, first, size) in enumerate(places):
        copies.append(
            pltpu.make_async_copy(
                source.at[pl.ds(first, size)], buffer.at[pl.ds(at, size)], sems.at[number]
            )
        )
        copies[-1].start()
        at += size
    for copy in copies:
        copy.wait()
    leaving = pltpu.make_async_copy(buffer, out_ref, sems.at[len(places)])
    leaving.start()
    leaving.wait()


def collect(pieces, part, extra):
    whole = 0 if extra is None else extra.shape[0]
    operands = list(pieces) + ([] if extra is None else [extra])
    count = 4 * len(pieces) + whole
    hbm = pl.BlockSpec(memory_space=pltpu.HBM)
    return pl.pallas_call(
        functools.partial(collect_kernel, part=part, whole=whole),
        out_shape=pltpu.HBM((count,) + pieces[0].shape[1:], pieces[0].dtype),
        in_specs=[hbm] * len(operands),
        out_specs=hbm,
        scratch_shapes=[
            pltpu.VMEM((count,) + pieces[0].shape[1:], pieces[0].dtype),
            pltpu.SemaphoreType.DMA((2 * len(pieces) + 2,)),
        ],
        name="collect_kept" if whole else "collect_swapped",
    )(*operands)


def finish_kernel(
    target_ref,
    wanted_ref,
    occupied_ref,
    fock_ref,
    energy_ref,
    energy_t_ref,
    fetched_ref,
    inter_ref,
    base_ref,
    own_ref,
    new_ref,
    second_ref,
    block_scr,
    inter_scr,
    base_scr,
    own_scr,
    new_scr,
    second_scr,
    in_sem,
    group_sem,
    out_sem,
    send_sem,
):
    pairs = own_scr.shape[0]
    last = send_sem is None
    groups = [(start, min(GROUP, pairs - start)) for start in range(0, pairs, GROUP)]
    waits = []
    for number, (start, size) in enumerate(groups):
        copies = [
            pltpu.make_async_copy(
                source.at[pl.ds(start, size)],
                buffer.at[pl.ds(start, size)],
                group_sem.at[kind, number],
            )
            for kind, (source, buffer) in enumerate(
                ((inter_ref, inter_scr), (own_ref, own_scr), (base_ref, base_scr))
            )
        ]
        for pair in range(start, start + size):
            copies.append(
                pltpu.make_async_copy(
                    fetched_ref.at[target_ref[pair]], block_scr.at[pair], in_sem.at[pair]
                )
            )
        for copy in copies:
            copy.start()
        waits.append(copies)
    leaving = []
    for number, (start, size) in enumerate(groups):
        for copy in waits[number]:
            copy.wait()
        group = range(start, start + size)
        firsts = [
            jnp.dot(inter_scr[pair], block_scr[pair], preferred_element_type=jnp.float32).astype(
                jnp.bfloat16
            )
            for pair in group
        ]
        terms = [
            lax.dot_general(
                first,
                inter_scr[pair],
                (((1,), (1,)), ((), ())),
                preferred_element_type=jnp.float32,
            )
            for pair, first in zip(group, firsts)
        ]
        for pair, term in zip(group, terms):
            denominator = (
                energy_t_ref[:, pair : pair + 1]
                + energy_ref[pair : pair + 1, :]
                - occupied_ref[pair]
            )
            residual = base_scr[pair] - fock_ref[pair] * term
            new = own_scr[pair].astype(jnp.float32) - residual / denominator
            new_scr[pair] = new.astype(jnp.bfloat16)
            if last:
                second_scr[pair] = residual.astype(jnp.bfloat16)
        results = [(new_scr, new_ref)] + ([(second_scr, second_ref)] if last else [])
        for kind, (buffer, out) in enumerate(results):
            leaving.append(
                pltpu.make_async_copy(
                    buffer.at[pl.ds(start, size)],
                    out.at[pl.ds(start, size)],
                    out_sem.at[kind, number],
                )
            )
            leaving[-1].start()
    if not last:
        for place in range(second_ref.shape[0]):
            leaving.append(
                pltpu.make_async_copy(
                    new_scr.at[wanted_ref[place]], second_ref.at[place], send_sem.at[place]
                )
            )
            leaving[-1].start()
    for copy in leaving:
        copy.wait()


def middle_kernel(*refs):
    finish_kernel(*refs[:17], None, *refs[17:])


def last_kernel(*refs):
    finish_kernel(*refs, None)


def finish(target, wanted, occupied, fock, fetched, inter, base, own, energy, last):
    pairs = own.shape[0]
    count = -(-pairs // GROUP)
    smem, vmem = pl.BlockSpec(memory_space=pltpu.SMEM), pl.BlockSpec(memory_space=pltpu.VMEM)
    hbm = pl.BlockSpec(memory_space=pltpu.HBM)
    narrow = pltpu.VMEM(own.shape, jnp.bfloat16)
    scratch = [narrow, narrow, pltpu.VMEM(own.shape, jnp.float32), narrow, narrow]
    if last:
        scratch.append(narrow)
    scratch += [
        pltpu.SemaphoreType.DMA((pairs,)),
        pltpu.SemaphoreType.DMA((3, count)),
        pltpu.SemaphoreType.DMA((2, count)),
    ]
    if not last:
        scratch.append(pltpu.SemaphoreType.DMA((fetched.shape[0],)))
    return pl.pallas_call(
        last_kernel if last else middle_kernel,
        out_shape=(
            pltpu.HBM(own.shape, jnp.bfloat16),
            pltpu.HBM(own.shape if last else fetched.shape, jnp.bfloat16),
        ),
        in_specs=[smem] * 4 + [vmem] * 2 + [hbm] * 4,
        out_specs=(hbm, hbm),
        scratch_shapes=scratch,
        name="finish_last" if last else "finish",
    )(target, wanted, occupied, fock, energy, energy.T, fetched, inter, base, own)


def body(
    amplitudes,
    exchange_ints,
    row_intersection,
    col_intersection,
    pno_energy,
    row_fock,
    col_fock,
    pair_occ,
    fock_occ,
    row_peer,
    row_slot,
    col_peer,
    col_slot,
):
    width = amplitudes.shape[1]
    row_capacity, col_capacity = 2, 3
    me = lax.axis_index("oj")
    col_rank = ranks(col_peer[:, 0])
    col_target = col_peer[:, 0] * col_capacity + col_rank
    col_table = request_table(col_peer[:, 0], col_slot, col_rank, lax.axis_size("oi"), col_capacity)
    col_wanted = lax.all_to_all(col_table, "oi", split_axis=0, concat_axis=0, tiled=True)
    row_wanted = row_requests(row_peer[:, 0], row_slot, me, row_capacity)
    near_wanted, far_wanted, row_target = row_plan(
        row_wanted, row_peer[:, 0], ranks(row_peer[:, 0]), me
    )
    matches = (
        pair_occ.reshape(-1)[:, None] == jnp.arange(fock_occ.shape[0], dtype=jnp.int32)[None, :]
    )
    picked = jnp.sum(jnp.where(matches, fock_occ[None, :], 0.0), axis=1).reshape(-1, 2)
    occupied = picked[:, 0] + picked[:, 1]
    denominator = pno_energy[:, :, None] + pno_energy[:, None, :] - occupied[:, None, None]
    ints_wide = exchange_ints.astype(jnp.float32)
    current = amplitudes
    col_send = current[col_wanted.reshape(-1)]
    for sweep in range(ITERS):
        col_fetched = lax.all_to_all(col_send, "oi", split_axis=0, concat_axis=0, tiled=True)
        row_fetched = row_exchange(current[near_wanted], current[far_wanted], width)
        row_term = couple(row_fetched[row_target], row_intersection)
        base = (
            ints_wide
            + denominator * current.astype(jnp.float32)
            - row_fock[:, None, None] * row_term
        )
        current, col_send = finish(
            col_target,
            col_wanted.reshape(-1),
            occupied,
            col_fock,
            col_fetched.reshape(-1, width, width),
            col_intersection,
            base,
            current,
            pno_energy,
            sweep == ITERS - 1,
        )
    return (current, col_send)


def solution(mesh):
    return jax.shard_map(
        body,
        mesh=mesh,
        in_specs=(
            P(("oi", "oj"), None, None),
            P(("oi", "oj"), None, None),
            P(("oi", "oj"), None, None),
            P(("oi", "oj"), None, None),
            P(("oi", "oj"), None),
            P(("oi", "oj")),
            P(("oi", "oj")),
            P(("oi", "oj"), None),
            P(),
            P(("oi", "oj"), None),
            P(("oi", "oj")),
            P(("oi", "oj"), None),
            P(("oi", "oj")),
        ),
        out_specs=(P(("oi", "oj"), None, None), P(("oi", "oj"), None, None)),
        check_vma=False,
    )
```
